32 devices in a mesh: ctx: 8 (over z, x), head: 4 (over y, core).
Axes of the slice: x: 2, y: 2, z: 4, core: 2. Of those that a mesh axis runs over, the one named last changes fastest.
Arguments:
- queries: bfloat16 [384, 5120], P('ctx', 'head'), as said below
- draft_keys: bfloat16 [384, 1024], P('ctx', 'head'), may hold values from -2.5 to 2.5
- draft_values: bfloat16 [384, 1024], P('ctx', 'head'), may hold values from -6 to 6
- cache_keys: bfloat16 [512, 128, 8, 128], P('ctx', None, 'head'), as said below
- cache_values: bfloat16 [512, 128, 8, 128], P('ctx', None, 'head'), may hold values from -6 to 6
- w_out: bfloat16 [5120, 5120], P('head', 'ctx'), may hold values from -0.078125 to 0.078125
- lengths: int32 [24], replicated, may hold values from 1 to 16384, as said below
- block_req: int32 [512], replicated, may hold values from 0 to 23, as said below
- block_idx: int32 [512], replicated, may hold values from -1 to 127
- move_dst: int32 [512], replicated, may hold values from -1 to 7, as said below
- draft_offs: int32 [24, 16], replicated, may hold values from 0 to 15, as said below
Outputs:
- mixed: bfloat16 [384, 5120], P('head', 'ctx')
- new_keys: bfloat16 [576, 128, 8, 128], P('ctx', None, 'head')
- new_values: bfloat16 [576, 128, 8, 128], P('ctx', None, 'head')
The draws below stay inside these ranges and needn't reach their ends.
Inputs may be any that keep to these rules, and one draw needn't show every extreme that they name: queries lie within -6 to 6. cache_keys lie within -6 to 6. Request r has exactly ceil(lengths[r] / 128) blocks, numbered from 0, each in exactly one slot. Empty slots hold block_req 0; on each index of ctx the live slots come before the empty ones. `move_dst`: only live blocks move, never to their own index; at most 2 blocks go from one index of ctx to one other and at most 8 arrive at one index, both reached. draft_offs[r, t] <= t.
All inputs are finite; a program needn't handle non-finite values.
Results may differ from the reference program's by a relative error of at most 0.0051.
Values may be sent and summed in bfloat16 or wider, within the bound.
A program may use at most 128 MiB of HBM per device.

```python
import math
import jax
import jax.numpy as jnp
from jax import lax

D = 5120
QH = 40
KVH = 8
HD = 128
GROUP = 5
DRAFT = 16
REQS = 24
BLK = 128
BLOCKS_DEV = 64
IN_DEV = 8
NBLK = 512
TOKENS = 384
N_CTX = 8


def draw_queries(key, part):
    values = jax.random.uniform(key, (TOKENS, QH * HD), jnp.float32, -6.0, 6.0)
    return values.astype(jnp.bfloat16)


def draw_cache_keys(key, part):
    values = jnp.clip(0.3 * jax.random.normal(key, (NBLK, BLK, KVH, HD), jnp.float32), -6.0, 6.0)
    return values.astype(jnp.bfloat16)


def plan_tables(key):
    base = jax.random.fold_in(key, 9173)
    keys = jax.random.split(base, 6)
    ndev = NBLK // BLOCKS_DEV
    half = ndev // 2
    devs = jnp.arange(ndev, dtype=jnp.int32)
    shuffled = jax.random.permutation(keys[0], ndev - 1).astype(jnp.int32)
    rank_of = jnp.full((ndev,), ndev - 1, jnp.int32).at[shuffled].set(jnp.arange(ndev - 1, dtype=jnp.int32))
    heavy = (rank_of < half).astype(jnp.int32)
    light = 1 - heavy
    receiver = jnp.sum(jnp.where(rank_of == half, devs, 0))
    low = jax.random.randint(keys[1], (ndev,), BLOCKS_DEV // 4, BLOCKS_DEV // 2 + 1).astype(jnp.int32)
    count = jnp.where(heavy == 1, BLOCKS_DEV, low).astype(jnp.int32)
    moves = jax.random.randint(keys[2], (ndev, ndev), 1, 3).astype(jnp.int32) * heavy[:, None] * light[None, :]
    moves = jnp.where((devs[None, :] == receiver) & (heavy[:, None] == 1), 2, moves).astype(jnp.int32)
    out_count = jnp.sum(moves, axis=1)
    cum = jnp.cumsum(moves, axis=1)
    slots = jnp.arange(BLOCKS_DEV, dtype=jnp.int32)
    offset = slots[None, :] - (count - out_count)[:, None]
    live = slots[None, :] < count[:, None]
    moved = (offset >= 0) & live
    dst = jnp.sum((cum[:, None, :] <= offset[:, :, None]).astype(jnp.int32), axis=2)
    move_dst = jnp.where(moved, dst, -1).astype(jnp.int32).reshape(-1)
    start_dev = jnp.cumsum(count) - count
    rank = start_dev[:, None] + slots[None, :]
    total = jnp.sum(count)
    longest = NBLK // 4
    reqs_line = jnp.arange(REQS, dtype=jnp.int32)
    long_id = jax.random.randint(keys[5], (), 0, REQS).astype(jnp.int32)
    is_long = reqs_line == long_id
    weights = jnp.where(is_long, 0, 1 + jax.random.randint(keys[3], (REQS,), 0, 2)).astype(jnp.int32)
    extra = total - longest - (REQS - 1)
    cum_in = jnp.cumsum(weights)
    cum_ex = cum_in - weights
    wsum = jnp.sum(weights)
    others = 1 + extra * cum_in // wsum - extra * cum_ex // wsum
    blocks_of = jnp.where(is_long, longest, others).astype(jnp.int32)
    start = jnp.cumsum(blocks_of) - blocks_of
    req = jnp.sum((start[None, None, :] <= rank[:, :, None]).astype(jnp.int32), axis=2) - 1
    req = jnp.clip(req, 0, REQS - 1)
    idx = rank - jnp.take(start, req)
    block_req = jnp.where(live, req, 0).astype(jnp.int32).reshape(-1)
    block_idx = jnp.where(live, idx, -1).astype(jnp.int32).reshape(-1)
    trim = jnp.where(is_long, 0, jax.random.randint(keys[4], (REQS,), 0, BLK - 1))
    lengths = (blocks_of * BLK - trim).astype(jnp.int32)
    return (lengths, block_req, block_idx, move_dst)


def draw_lengths(key, part):
    return plan_tables(key)[0]


def draw_block_req(key, part):
    return plan_tables(key)[1]


def draw_block_idx(key, part):
    return plan_tables(key)[2]


def draw_move_dst(key, part):
    return plan_tables(key)[3]


def draw_draft_offs(key, part):
    base = jax.random.fold_in(key, 3307)
    tpos = jnp.arange(DRAFT, dtype=jnp.int32)
    offs = jax.random.randint(base, (REQS, DRAFT), 0, tpos[None, :] + 1).astype(jnp.int32)
    return offs.at[0, DRAFT - 1].set(DRAFT - 1)


def block_levels(stream_key, shape, cuts, low, high):
    def one(position, parts):
        steps = jax.random.uniform(jax.random.fold_in(jax.random.fold_in(stream_key, 6), position), (parts,), jnp.float32, low / len(cuts), high / len(cuts))
        return jnp.repeat(jnp.exp(steps), shape[position] // parts).reshape((-1,) + (1,) * (len(shape) - position - 1))

    level = one(*cuts[0])
    for cut in cuts[1:]:
        level = level * one(*cut)
    return level


def gaussian(key, dims, scale, limit, shards=(), held_as=jnp.bfloat16):
    result = jax.random.normal(key, dims, jnp.float32) * scale
    if len(shards) > 0:
        result = block_levels(key, dims, shards, -0.22, 0.18) * result
    return jnp.clip(result, min=-limit, max=limit).astype(held_as)


def setup_inputs(seed: int = 0) -> dict:
    arg_keys = jax.random.split(jax.random.key(seed), 12)
    return {
        "queries": draw_queries(jax.random.fold_in(arg_keys[11], 71), 0),
        "draft_keys": gaussian(arg_keys[1], (TOKENS, KVH * HD), 0.3, 2.5, ((0, 8), (1, 4))),
        "draft_values": gaussian(arg_keys[2], (TOKENS, KVH * HD), 1.0, 6.0, ((0, 8), (1, 4))),
        "cache_keys": draw_cache_keys(jax.random.fold_in(arg_keys[11], 71), 0),
        "cache_values": gaussian(arg_keys[4], (NBLK, BLK, KVH, HD), 1.0, 6.0, ((0, 8), (2, 4))),
        "w_out": gaussian(arg_keys[5], (QH * HD, D), (QH * HD) ** -0.5, 0.078125, ((0, 4), (1, 8))),
        "lengths": draw_lengths(jax.random.fold_in(arg_keys[11], 71), 0),
        "block_req": draw_block_req(jax.random.fold_in(arg_keys[11], 71), 0),
        "block_idx": draw_block_idx(jax.random.fold_in(arg_keys[11], 71), 0),
        "move_dst": draw_move_dst(jax.random.fold_in(arg_keys[11], 71), 0),
        "draft_offs": draw_draft_offs(jax.random.fold_in(arg_keys[11], 71), 0),
    }


def live_tokens(lengths, block_req, block_idx):
    own_len = jnp.take(lengths, block_req) - block_idx * BLK
    counts = jnp.where(block_idx >= 0, jnp.clip(own_len, 0, BLK), 0)
    return jnp.arange(BLK, dtype=jnp.int32)[None, :] < counts[:, None]

def draft_seen(draft_offs):
    tpos = jnp.arange(DRAFT, dtype=jnp.int32)
    return (tpos[None, None, :] >= draft_offs[:, :, None]) & (tpos[None, None, :] <= tpos[None, :, None])

def relocate(cache, move_dst):
    every = jnp.arange(NBLK, dtype=jnp.int32)
    moved = move_dst >= 0
    earlier = (move_dst[:, None] == move_dst[None, :]) & (every[None, :] < every[:, None])
    order = lax.optimization_barrier(jnp.sum(earlier.astype(jnp.int32), axis=1))
    width = BLOCKS_DEV + IN_DEV
    home = every // BLOCKS_DEV * width + every % BLOCKS_DEV
    away = jnp.where(moved, move_dst * width + BLOCKS_DEV + order, N_CTX * width)
    kept = jnp.where(moved[:, None, None, None], jnp.zeros_like(cache), cache)
    fresh = jnp.zeros((N_CTX * width,) + cache.shape[1:], cache.dtype)
    fresh = fresh.at[home].set(kept)
    return fresh.at[away].set(cache, mode='drop')

def reference(queries, draft_keys, draft_values, cache_keys, cache_values, w_out, lengths, block_req, block_idx, move_dst, draft_offs):
    scale = 1.0 / math.sqrt(HD)
    live = live_tokens(lengths, block_req, block_idx)
    seen = draft_seen(draft_offs)
    onehot = block_req[None, :] == jnp.arange(REQS, dtype=jnp.int32)[:, None]
    onehot_f = onehot.astype(jnp.float32)
    q_heads = jnp.transpose(queries.reshape(REQS, DRAFT, KVH, GROUP, HD), (2, 0, 1, 3, 4))
    k_heads = jnp.transpose(cache_keys, (2, 0, 1, 3))
    v_heads = jnp.transpose(cache_values, (2, 0, 1, 3))
    dk_heads = jnp.transpose(draft_keys.reshape(REQS, DRAFT, KVH, HD), (2, 0, 1, 3))
    dv_heads = jnp.transpose(draft_values.reshape(REQS, DRAFT, KVH, HD), (2, 0, 1, 3))

    def one_head(items):
        q_one, k_one, v_one, dk_one, dv_one = items
        q_slot = jnp.take(q_one, block_req, axis=0)
        scores = jnp.einsum('btgd,bjd->btgj', q_slot.astype(jnp.float32), k_one.astype(jnp.float32)) * scale
        scores = jnp.where(live[:, None, None, :], scores, -jnp.inf)
        block_top = lax.optimization_barrier(jnp.max(scores, axis=3))
        cache_top = lax.optimization_barrier(jnp.max(jnp.where(onehot[:, :, None, None], block_top[None], -jnp.inf), axis=1))
        dscores = jnp.einsum('rtgd,rud->rtgu', q_one.astype(jnp.float32), dk_one.astype(jnp.float32)) * scale
        dscores = jnp.where(seen[:, :, None, :], dscores, -jnp.inf)
        top = jnp.maximum(cache_top, lax.optimization_barrier(jnp.max(dscores, axis=3)))
        probs = jnp.where(live[:, None, None, :], jnp.exp(scores - jnp.take(top, block_req, axis=0)[..., None]), 0.0)
        dprobs = jnp.where(seen[:, :, None, :], jnp.exp(dscores - top[..., None]), 0.0)
        denom = jnp.einsum('rb,btg->rtg', onehot_f, lax.optimization_barrier(jnp.sum(probs, axis=3)), precision=lax.Precision.HIGHEST) + lax.optimization_barrier(jnp.sum(dprobs, axis=3))
        pbf = probs.astype(jnp.bfloat16).astype(jnp.float32)
        slot_numer = jnp.einsum('btgj,bjd->btgd', pbf, v_one.astype(jnp.float32))
        numer = jnp.einsum('rb,btgd->rtgd', onehot_f, slot_numer, precision=lax.Precision.HIGHEST)
        dpbf = dprobs.astype(jnp.bfloat16).astype(jnp.float32)
        numer = numer + jnp.einsum('rtgu,rud->rtgd', dpbf, dv_one.astype(jnp.float32))
        return (numer / denom[..., None]).astype(jnp.bfloat16)
    heads_out = lax.map(one_head, (q_heads, k_heads, v_heads, dk_heads, dv_heads))
    attn = jnp.transpose(heads_out, (1, 2, 0, 3, 4)).reshape(TOKENS, QH * HD)
    mixed = jnp.dot(attn, w_out, preferred_element_type=jnp.float32).astype(jnp.bfloat16)
    return (mixed, relocate(cache_keys, move_dst), relocate(cache_values, move_dst))
```

```python
import functools
import math

import jax
import jax.numpy as jnp
from jax import lax
from jax.experimental import pallas as pl
from jax.experimental.pallas import tpu as pltpu
from jax.sharding import PartitionSpec as P

CAP = 2
STEP = 8
TOGETHER = 4
NEG = -1e30
MESH = pl.DeviceIdType.MESH
VMEM = pl.BlockSpec(memory_space=pltpu.VMEM)
SMEM = pl.BlockSpec(memory_space=pltpu.SMEM)
ANY = pl.BlockSpec(memory_space=pl.ANY)


def greet(axes):
    barrier = pltpu.get_barrier_semaphore()
    total = 0
    for axis, size in axes:
        me = lax.axis_index(axis)
        for d in range(1, size):
            pl.semaphore_signal(
                barrier, inc=1, device_id={axis: lax.rem(me + d, size)}, device_id_type=MESH
            )
        total += size - 1
    pl.semaphore_wait(barrier, total)


def remote(src, dst, send, recv, axis, to):
    return pltpu.make_async_remote_copy(
        src_ref=src, dst_ref=dst, send_sem=send, recv_sem=recv, device_id={axis: to}, device_id_type=MESH
    )


def spread(n, parts, send_sem, recv_sem, pair_send, pair_recv):
    me = lax.axis_index("ctx")
    half = n // 2
    row, side = me // 2, lax.rem(me, 2)
    partner = row * 2 + 1 - side
    started = []
    for a, (src, dst) in enumerate(parts):
        for d in range(1, half):
            to = lax.rem(row + d, half) * 2 + side
            c = remote(src, dst.at[me], send_sem.at[a, d], recv_sem.at[a, d], "ctx", to)
            c.start()
            started.append(c)
        c = remote(src, dst.at[me], pair_send.at[a, 0], pair_recv.at[a, 0], "ctx", partner)
        c.start()
        started.append(c)
    for d in range(1, half):
        for a, (src, dst) in enumerate(parts):
            origin = lax.rem(row + half - d, half) * 2 + side
            remote(src, dst.at[origin], send_sem.at[a, d], recv_sem.at[a, d], "ctx", partner).wait_recv()
            c = remote(
                dst.at[origin], dst.at[origin], pair_send.at[a, d], pair_recv.at[a, d], "ctx", partner
            )
            c.start()
            started.append(c)
    for d in range(half):
        for a, (src, dst) in enumerate(parts):
            origin = lax.rem(row + half - d, half) * 2 + 1 - side
            remote(src, dst.at[origin], pair_send.at[a, d], pair_recv.at[a, d], "ctx", partner).wait_recv()
    for c in started:
        c.wait_send()


def spread_sems(n, count):
    half = n // 2
    return [pltpu.SemaphoreType.DMA((count, half))] * 4


def gather_kernel(n, count, *refs):
    srcs, dsts, sems = refs[:count], refs[count : 2 * count], refs[2 * count :]
    local = sems[4]
    greet([("ctx", n)])
    me = lax.axis_index("ctx")
    own = []
    for a in range(count):
        c = pltpu.make_async_copy(srcs[a], dsts[a].at[me], local.at[a])
        c.start()
        own.append(c)
    spread(n, list(zip(srcs, dsts)), *sems[:4])
    for c in own:
        c.wait()


def gather_all(n, arrays):
    count = len(arrays)
    return pl.pallas_call(
        functools.partial(gather_kernel, n, count),
        out_shape=[jax.ShapeDtypeStruct((n,) + x.shape, x.dtype) for x in arrays],
        in_specs=[VMEM] * count,
        out_specs=[VMEM] * count,
        scratch_shapes=spread_sems(n, count) + [pltpu.SemaphoreType.DMA((count,))],
        compiler_params=pltpu.CompilerParams(collective_id=0, has_side_effects=True),
        name="gather_queries",
    )(*arrays)


def pack_kernel(blocks, n, rank_ref, dst_ref, k_ref, v_ref, out_ref, seen, sem):
    base = rank_ref[0] * blocks
    for d in range(n):
        seen[d] = 0

    def start(s, _):
        d = dst_ref[base + s]

        @pl.when(d >= 0)
        def _():
            row = d * CAP + seen[d]
            seen[d] = seen[d] + 1
            pltpu.make_async_copy(k_ref.at[s], out_ref.at[row, 0], sem).start()
            pltpu.make_async_copy(v_ref.at[s], out_ref.at[row, 1], sem).start()

        return 0

    lax.fori_loop(0, blocks, start, 0)

    def finish(s, _):
        @pl.when(dst_ref[base + s] >= 0)
        def _():
            pltpu.make_async_copy(k_ref.at[0], out_ref.at[0, 0], sem).wait()
            pltpu.make_async_copy(v_ref.at[0], out_ref.at[0, 1], sem).wait()

        return 0

    lax.fori_loop(0, blocks, finish, 0)


def pack(n, rank, move_dst, keys, values):
    blocks, rows, lanes = keys.shape
    return pl.pallas_call(
        functools.partial(pack_kernel, blocks, n),
        out_shape=jax.ShapeDtypeStruct((n * CAP, 2, rows, lanes), keys.dtype),
        in_specs=[SMEM, SMEM, ANY, ANY],
        out_specs=VMEM,
        scratch_shapes=[pltpu.SMEM((n,), jnp.int32), pltpu.SemaphoreType.DMA],
        name="pack_moves",
    )(rank, move_dst, keys, values)


def unpack_kernel(blocks, n, cnt_ref, recv_ref, nk_in, nv_in, nk_ref, nv_ref, stage, at, sem, out_sem):
    at[0] = 0
    for src in range(n):
        for j in range(CAP):

            @pl.when((j < cnt_ref[src]) & (at[0] < n))
            def _():
                for a in range(2):
                    pltpu.make_async_copy(
                        recv_ref.at[src * CAP + j, a], stage.at[a, at[0]], sem
                    ).start()
                at[0] = at[0] + 1

    total = at[0]

    def blank(k, _):
        stage[:, k] = jnp.zeros_like(stage[:, k])
        return 0

    lax.fori_loop(total, n, blank, 0)

    def finish(k, _):
        for a in range(2):
            pltpu.make_async_copy(recv_ref.at[0, a], stage.at[a, 0], sem).wait()
        return 0

    lax.fori_loop(0, total, finish, 0)
    outs = [
        pltpu.make_async_copy(stage.at[a], ref.at[pl.ds(blocks, n)], out_sem.at[a])
        for a, ref in enumerate((nk_ref, nv_ref))
    ]
    for c in outs:
        c.start()
    for c in outs:
        c.wait()


def unpack(n, blocks, arriving, received, new_keys, new_values):
    rows, lanes = new_keys.shape[1:]
    return pl.pallas_call(
        functools.partial(unpack_kernel, blocks, n),
        out_shape=[jax.ShapeDtypeStruct(x.shape, x.dtype) for x in (new_keys, new_values)],
        in_specs=[SMEM, ANY, ANY, ANY],
        out_specs=[ANY, ANY],
        input_output_aliases={2: 0, 3: 1},
        scratch_shapes=[
            pltpu.VMEM((2, n, rows, lanes), new_keys.dtype),
            pltpu.SMEM((1,), jnp.int32),
            pltpu.SemaphoreType.DMA,
            pltpu.SemaphoreType.DMA((2,)),
        ],
        name="place_moves",
    )(arriving, received, new_keys, new_values)


def attend_kernel(
    dims,
    rank_ref,
    req_ref,
    idx_ref,
    dst_ref,
    len_ref,
    dreq_ref,
    q_ref,
    k_ref,
    v_ref,
    dk_ref,
    dv_ref,
    bias_ref,
    nk_ref,
    nv_ref,
    o_ref,
    lse_ref,
    tok_ref,
    acc,
    top,
    den,
):
    blocks, width, kv, heads, hd, drafts, requests, own, aligned, steps = dims
    group = heads // kv
    qrows = heads * drafts
    i = pl.program_id(0)
    base = rank_ref[0] * blocks + i * STEP
    factor = math.log2(math.e) / math.sqrt(hd)
    nt = (((1,), (1,)), ((), ()))

    def query(r):
        q = q_ref[pl.ds(pl.multiple_of(r * drafts, drafts), drafts), :]
        return jnp.concatenate([q[:, h * hd : (h + 1) * hd] for h in range(heads)], axis=0)

    def part(s, v):
        m = jnp.max(s, axis=1, keepdims=True)
        p = jnp.exp2(s - m)
        total = jnp.sum(p, axis=1, keepdims=True)
        o = jnp.dot(p.astype(jnp.bfloat16), v, preferred_element_type=jnp.float32)
        return m, total, o

    def merge(r, m, total, o):
        old = top[r]
        new = jnp.maximum(old, m)
        a, b = jnp.exp2(old - new), jnp.exp2(m - new)
        top[r] = new
        den[r] = den[r] * a + total * b
        acc[r] = acc[r] * a + o * b

    @pl.when(i == 0)
    def _():
        row = lax.broadcasted_iota(jnp.int32, (qrows, kv * width), 0)
        col = lax.broadcasted_iota(jnp.int32, (qrows, kv * width), 1)
        tok_ref[...] = jnp.where(row // (group * drafts) == col % kv, col // kv, width)
        top[...] = jnp.full_like(top, NEG)
        den[...] = jnp.zeros_like(den)
        acc[...] = jnp.zeros_like(acc)
        for x in range(own):
            r = dreq_ref[x]
            place = x * drafts if aligned else pl.multiple_of(r * drafts, drafts)
            dk = dk_ref[pl.ds(place, drafts), :]
            dv = dv_ref[pl.ds(place, drafts), :]
            dk = jnp.concatenate([dk[:, g * hd : (g + 1) * hd] for g in range(kv)], axis=0)
            dv = jnp.concatenate([dv[:, g * hd : (g + 1) * hd] for g in range(kv)], axis=0)
            s = lax.dot_general(query(r), dk, nt, preferred_element_type=jnp.float32) * factor
            merge(r, *part(jnp.where(bias_ref[x] < 0, NEG, s), dv))

    for lo in range(0, STEP, TOGETHER):
        found = []
        for b in range(lo, lo + TOGETHER):
            r, x = req_ref[base + b], idx_ref[base + b]
            count = jnp.where(x >= 0, jnp.clip(len_ref[r] - x * width, 0, width), 0)
            s = lax.dot_general(query(r), k_ref[b], nt, preferred_element_type=jnp.float32) * factor
            s = jnp.where(tok_ref[...] < count, s, NEG)
            found.append((r,) + part(s, v_ref[b]))
        for r, m, total, o in found:
            merge(r, m, total, o)
    for b in range(STEP):
        away = dst_ref[base + b] >= 0

        @pl.when(away)
        def _():
            nk_ref[b] = jnp.zeros_like(nk_ref[b])
            nv_ref[b] = jnp.zeros_like(nv_ref[b])

        @pl.when(jnp.logical_not(away))
        def _():
            nk_ref[b] = k_ref[b]
            nv_ref[b] = v_ref[b]

    @pl.when(i == steps - 1)
    def _():
        lane = lax.broadcasted_iota(jnp.int32, (drafts, hd), 1)
        if o_ref.shape[0] > requests * drafts:
            rest = pl.ds(requests * drafts, o_ref.shape[0] - requests * drafts)
            o_ref[rest, :] = jnp.zeros_like(o_ref[rest, :])
            lse_ref[rest, :] = jnp.zeros_like(lse_ref[rest, :])

        def close(r, _):
            m, total = top[r], den[r]
            dead = total <= 0
            o = acc[r] * jnp.where(dead, 0.0, 1.0 / jnp.where(dead, 1.0, total))
            level = jnp.where(dead, NEG, m + jnp.log2(jnp.where(dead, 1.0, total)))
            rows = pl.ds(pl.multiple_of(r * drafts, drafts), drafts)
            packed = jnp.full((drafts, hd), NEG, jnp.float32)
            for h in range(heads):
                o_ref[rows, h * hd : (h + 1) * hd] = o[h * drafts : (h + 1) * drafts].astype(jnp.bfloat16)
                packed = jnp.where(lane == h, level[h * drafts : (h + 1) * drafts], packed)
            lse_ref[rows, :] = packed
            return 0

        lax.fori_loop(0, requests, close, 0)


def attend(n, rank, tables, dreq, q_all, keys, values, dk, dv, bias, kv, drafts, out_rows, aligned):
    blocks, rows, hd = keys.shape
    width = rows // kv
    block_req, block_idx, move_dst, lengths = tables
    requests = lengths.shape[0]
    heads = q_all.shape[1] // hd
    steps = blocks // STEP
    qrows = heads * drafts
    own = bias.shape[0]
    dims = (blocks, width, kv, heads, hd, drafts, requests, own, aligned, steps)
    whole = lambda x: pl.BlockSpec(x.shape, lambda i, *_: (0,) * x.ndim)
    slab = pl.BlockSpec((STEP, rows, hd), lambda i, *_: (i, 0, 0))
    grown = jax.ShapeDtypeStruct((blocks + n, rows, hd), keys.dtype)
    o = jax.ShapeDtypeStruct((out_rows, heads * hd), jnp.bfloat16)
    lse = jax.ShapeDtypeStruct((out_rows, hd), jnp.float32)
    return pl.pallas_call(
        functools.partial(attend_kernel, dims),
        out_shape=[grown, grown, o, lse],
        grid_spec=pltpu.PrefetchScalarGridSpec(
            num_scalar_prefetch=6,
            grid=(steps,),
            in_specs=[whole(q_all), slab, slab, whole(dk), whole(dv), whole(bias)],
            out_specs=[slab, slab, whole(o), whole(lse)],
            scratch_shapes=[
                pltpu.VMEM((qrows, rows), jnp.int32),
                pltpu.VMEM((requests, qrows, hd), jnp.float32),
                pltpu.VMEM((requests, qrows, hd), jnp.float32),
                pltpu.VMEM((requests, qrows, hd), jnp.float32),
            ],
        ),
        compiler_params=pltpu.CompilerParams(dimension_semantics=("arbitrary",)),
        cost_estimate=pl.CostEstimate(
            flops=4 * blocks * qrows * rows * hd, bytes_accessed=8 * blocks * rows * hd, transcendentals=0
        ),
        name="attend",
    )(rank, block_req, block_idx, move_dst, lengths, dreq, q_all, keys, values, dk, dv, bias)


def combine_kernel(dims, o_ref, lse_ref, w_ref, out_ref, got_o, got_l, attn_own, attn, part, got, *sems):
    n, nh, chunk, heads, hd, chunks, rows = dims
    os, orv, ls, lrv, hs, hr = sems[:6]
    local = sems[10]
    me = lax.axis_index("ctx")
    hme = lax.axis_index("head")
    greet([("ctx", n), ("head", nh)])
    sends = []
    for d in range(1, n):
        to = lax.rem(me + d, n)
        for src, dst, ss, rs in ((lse_ref, got_l, ls, lrv), (o_ref, got_o, os, orv)):
            c = remote(src.at[to], dst.at[d], ss.at[d], rs.at[d], "ctx", to)
            c.start()
            sends.append(c)
    for c in sends:
        c.wait_recv()
    levels = [lse_ref[me]] + [got_l[d] for d in range(1, n)]
    best = functools.reduce(jnp.maximum, levels)
    weights = [jnp.exp2(x - best) for x in levels]
    norm = 1.0 / functools.reduce(jnp.add, weights)
    weights = [x * norm for x in weights]
    for h in range(heads):
        cols = slice(h * hd, (h + 1) * hd)
        total = weights[0][:, h : h + 1] * o_ref[me, :, cols].astype(jnp.float32)
        for d in range(1, n):
            total += weights[d][:, h : h + 1] * got_o[d, :, cols].astype(jnp.float32)
        attn_own[:, cols] = total.astype(jnp.bfloat16)
    mine = pltpu.make_async_copy(attn_own, attn.at[me], local)
    mine.start()
    spread(n, [(attn_own, attn)], *sems[6:10])
    mine.wait()
    for c in sends:
        c.wait_send()
    w = w_ref[...]
    sends = []
    for d in range(1, nh):
        to = lax.rem(hme + d, nh)
        start = pl.multiple_of(to * rows, 16)
        part[d] = jnp.dot(
            attn_rows(attn, start, rows, chunk), w, preferred_element_type=jnp.float32
        ).astype(jnp.bfloat16)
        c = remote(part.at[d], got.at[d], hs.at[d], hr.at[d], "head", to)
        c.start()
        sends.append(c)
    total = jnp.dot(
        attn_rows(attn, pl.multiple_of(hme * rows, 16), rows, chunk), w, preferred_element_type=jnp.float32
    )
    for c in sends:
        c.wait_recv()
    for d in range(1, nh):
        total += got[d].astype(jnp.float32)
    out_ref[...] = total.astype(jnp.bfloat16)
    for c in sends:
        c.wait_send()


def attn_rows(attn, start, rows, chunk):
    piece = math.gcd(rows, chunk)
    out = []
    for x in range(rows // piece):
        at = start + x * piece
        out.append(attn[at // chunk, pl.ds(pl.multiple_of(lax.rem(at, chunk), 16), piece), :])
    return jnp.concatenate(out, axis=0)


def combine(n, nh, o, lse, w, tokens):
    _, chunk, cols = o.shape
    hd = lse.shape[2]
    heads = cols // hd
    rows = tokens // nh
    wide = w.shape[1]
    dims = (n, nh, chunk, heads, hd, tokens // chunk, rows)
    dma = pltpu.SemaphoreType.DMA
    return pl.pallas_call(
        functools.partial(combine_kernel, dims),
        out_shape=jax.ShapeDtypeStruct((rows, wide), jnp.bfloat16),
        in_specs=[VMEM] * 3,
        out_specs=VMEM,
        scratch_shapes=[
            pltpu.VMEM((n, chunk, cols), jnp.bfloat16),
            pltpu.VMEM((n, chunk, hd), jnp.float32),
            pltpu.VMEM((chunk, cols), jnp.bfloat16),
            pltpu.VMEM((n, chunk, cols), jnp.bfloat16),
            pltpu.VMEM((nh, rows, wide), jnp.bfloat16),
            pltpu.VMEM((nh, rows, wide), jnp.bfloat16),
            dma((n,)),
            dma((n,)),
            dma((n,)),
            dma((n,)),
            dma((nh,)),
            dma((nh,)),
        ]
        + spread_sems(n, 1)
        + [dma],
        compiler_params=pltpu.CompilerParams(collective_id=1, has_side_effects=True),
        name="combine",
    )(o, lse, w)


def shards(
    n,
    nh,
    queries,
    draft_keys,
    draft_values,
    cache_keys,
    cache_values,
    w_out,
    lengths,
    block_req,
    block_idx,
    move_dst,
    draft_offs,
):
    blocks, width, kv, hd = cache_keys.shape
    requests, drafts = draft_offs.shape
    tokens = requests * drafts
    local_tokens = queries.shape[0]
    heads = queries.shape[1] // hd
    me = lax.axis_index("ctx")
    rank = jnp.reshape(me, (1,)).astype(jnp.int32)
    keys = cache_keys.reshape(blocks, width * kv, hd)
    values = cache_values.reshape(blocks, width * kv, hd)
    sent = pack(n, rank, move_dst, keys, values)
    received = lax.all_to_all(sent, "ctx", split_axis=0, concat_axis=0, tiled=True)
    arriving = jnp.sum((move_dst.reshape(n, blocks) == me).astype(jnp.int32), axis=1)

    aligned = local_tokens % drafts == 0
    if aligned:
        own = local_tokens // drafts
        dreq = me * own + jnp.arange(own, dtype=jnp.int32)
        valid = jnp.full((own,), True)
        (q_all,) = gather_all(n, [queries])
        dk, dv = draft_keys, draft_values
    else:
        own = -(-requests // n)
        dreq = me + n * jnp.arange(own, dtype=jnp.int32)
        valid = dreq < requests
        dreq = jnp.where(valid, dreq, 0)
        q_all, dk, dv = gather_all(n, [queries, draft_keys, draft_values])
        dk, dv = dk.reshape(tokens, -1), dv.reshape(tokens, -1)
    q_all = q_all.reshape(tokens, heads * hd)
    offs = jnp.take(draft_offs, dreq, axis=0)
    line = jnp.arange(drafts, dtype=jnp.int32)
    seen = (line[None, None, :] >= offs[:, :, None]) & (line[None, None, :] <= line[None, :, None])
    seen = seen & valid[:, None, None]
    same = jnp.arange(heads)[:, None] // (heads // kv) == jnp.arange(kv)[None, :]
    bias = jnp.where(
        seen[:, None, :, None, :] & same[None, :, None, :, None], 0.0, -1.0
    ).astype(jnp.float32).reshape(own, heads * drafts, kv * drafts)
    chunk = -(-requests // n) * drafts
    new_keys, new_values, o, lse = attend(
        n,
        rank,
        (block_req, block_idx, move_dst, lengths),
        dreq,
        q_all,
        keys,
        values,
        dk,
        dv,
        bias,
        kv,
        drafts,
        n * chunk,
        aligned,
    )
    mixed = combine(n, nh, o.reshape(n, chunk, -1), lse.reshape(n, chunk, -1), w_out, tokens)
    new_keys, new_values = unpack(n, blocks, arriving, received, new_keys, new_values)
    shape = (blocks + n, width, kv, hd)
    return (mixed, new_keys.reshape(shape), new_values.reshape(shape))


def solution(mesh):
    in_specs = (
        P("ctx", "head"),
        P("ctx", "head"),
        P("ctx", "head"),
        P("ctx", None, "head", None),
        P("ctx", None, "head", None),
        P("head", "ctx"),
        P(),
        P(),
        P(),
        P(),
        P(),
    )
    out_specs = (P("head", "ctx"), P("ctx", None, "head", None), P("ctx", None, "head", None))
    body = functools.partial(shards, mesh.shape["ctx"], mesh.shape["head"])
    return jax.shard_map(body, mesh=mesh, in_specs=in_specs, out_specs=out_specs, check_vma=False)
```

```python
import functools
import math

import jax
import jax.numpy as jnp
from jax import lax
from jax.experimental import pallas as pl
from jax.experimental.pallas import tpu as pltpu
from jax.sharding import PartitionSpec as P

CAP = 2
STEP = 8
TOGETHER = 4
NEG = -1e30
MESH = pl.DeviceIdType.MESH
VMEM = pl.BlockSpec(memory_space=pltpu.VMEM)
SMEM = pl.BlockSpec(memory_space=pltpu.SMEM)
ANY = pl.BlockSpec(memory_space=pl.ANY)


def greet(axes):
    barrier = pltpu.get_barrier_semaphore()
    total = 0
    for axis, size in axes:
        me = lax.axis_index(axis)
        for d in range(1, size):
            pl.semaphore_signal(
                barrier, inc=1, device_id={axis: lax.rem(me + d, size)}, device_id_type=MESH
            )
        total += size - 1
    pl.semaphore_wait(barrier, total)


def remote(src, dst, send, recv, axis, to):
    return pltpu.make_async_remote_copy(
        src_ref=src, dst_ref=dst, send_sem=send, recv_sem=recv, device_id={axis: to}, device_id_type=MESH
    )


def spread(n, parts, send_sem, recv_sem, pair_send, pair_recv):
    me = lax.axis_index("ctx")
    half = n // 2
    row, side = me // 2, lax.rem(me, 2)
    partner = row * 2 + 1 - side
    started = []
    for a, (src, dst) in enumerate(parts):
        for d in range(1, half):
            to = lax.rem(row + d, half) * 2 + side
            c = remote(src, dst.at[me], send_sem.at[a, d], recv_sem.at[a, d], "ctx", to)
            c.start()
            started.append(c)
        c = remote(src, dst.at[me], pair_send.at[a, 0], pair_recv.at[a, 0], "ctx", partner)
        c.start()
        started.append(c)
    for d in range(1, half):
        for a, (src, dst) in enumerate(parts):
            origin = lax.rem(row + half - d, half) * 2 + side
            remote(src, dst.at[origin], send_sem.at[a, d], recv_sem.at[a, d], "ctx", partner).wait_recv()
            c = remote(
                dst.at[origin], dst.at[origin], pair_send.at[a, d], pair_recv.at[a, d], "ctx", partner
            )
            c.start()
            started.append(c)
    for d in range(half):
        for a, (src, dst) in enumerate(parts):
            origin = lax.rem(row + half - d, half) * 2 + 1 - side
            remote(src, dst.at[origin], pair_send.at[a, d], pair_recv.at[a, d], "ctx", partner).wait_recv()
    for c in started:
        c.wait_send()


def spread_sems(n, count):
    half = n // 2
    return [pltpu.SemaphoreType.DMA((count, half))] * 4


def gather_kernel(n, count, *refs):
    srcs, dsts, sems = refs[:count], refs[count : 2 * count], refs[2 * count :]
    local = sems[4]
    greet([("ctx", n)])
    me = lax.axis_index("ctx")
    own = []
    for a in range(count):
        c = pltpu.make_async_copy(srcs[a], dsts[a].at[me], local.at[a])
        c.start()
        own.append(c)
    spread(n, list(zip(srcs, dsts)), *sems[:4])
    for c in own:
        c.wait()


def gather_all(n, arrays):
    count = len(arrays)
    return pl.pallas_call(
        functools.partial(gather_kernel, n, count),
        out_shape=[jax.ShapeDtypeStruct((n,) + x.shape, x.dtype) for x in arrays],
        in_specs=[VMEM] * count,
        out_specs=[VMEM] * count,
        scratch_shapes=spread_sems(n, count) + [pltpu.SemaphoreType.DMA((count,))],
        compiler_params=pltpu.CompilerParams(collective_id=0, has_side_effects=True),
        name="gather_queries",
    )(*arrays)


def pack_kernel(blocks, n, rank_ref, dst_ref, k_ref, v_ref, out_ref, seen, sem):
    base = rank_ref[0] * blocks
    for d in range(n):
        seen[d] = 0

    def start(s, _):
        d = dst_ref[base + s]

        @pl.when(d >= 0)
        def _():
            row = d * CAP + seen[d]
            seen[d] = seen[d] + 1
            pltpu.make_async_copy(k_ref.at[s], out_ref.at[row, 0], sem).start()
            pltpu.make_async_copy(v_ref.at[s], out_ref.at[row, 1], sem).start()

        return 0

    lax.fori_loop(0, blocks, start, 0)

    def finish(s, _):
        @pl.when(dst_ref[base + s] >= 0)
        def _():
            pltpu.make_async_copy(k_ref.at[0], out_ref.at[0, 0], sem).wait()
            pltpu.make_async_copy(v_ref.at[0], out_ref.at[0, 1], sem).wait()

        return 0

    lax.fori_loop(0, blocks, finish, 0)


def pack(n, rank, move_dst, keys, values):
    blocks, rows, lanes = keys.shape
    return pl.pallas_call(
        functools.partial(pack_kernel, blocks, n),
        out_shape=jax.ShapeDtypeStruct((n * CAP, 2, rows, lanes), keys.dtype),
        in_specs=[SMEM, SMEM, ANY, ANY],
        out_specs=VMEM,
        scratch_shapes=[pltpu.SMEM((n,), jnp.int32), pltpu.SemaphoreType.DMA],
        name="pack_moves",
    )(rank, move_dst, keys, values)


def unpack_kernel(blocks, n, cnt_ref, recv_ref, nk_in, nv_in, nk_ref, nv_ref, stage, at, sem, out_sem):
    at[0] = 0
    for src in range(n):
        for j in range(CAP):

            @pl.when((j < cnt_ref[src]) & (at[0] < n))
            def _():
                for a in range(2):
                    pltpu.make_async_copy(
                        recv_ref.at[src * CAP + j, a], stage.at[a, at[0]], sem
                    ).start()
                at[0] = at[0] + 1

    total = at[0]

    def blank(k, _):
        stage[:, k] = jnp.zeros_like(stage[:, k])
        return 0

    lax.fori_loop(total, n, blank, 0)

    def finish(k, _):
        for a in range(2):
            pltpu.make_async_copy(recv_ref.at[0, a], stage.at[a, 0], sem).wait()
        return 0

    lax.fori_loop(0, total, finish, 0)
    outs = [
        pltpu.make_async_copy(stage.at[a], ref.at[pl.ds(blocks, n)], out_sem.at[a])
        for a, ref in enumerate((nk_ref, nv_ref))
    ]
    for c in outs:
        c.start()
    for c in outs:
        c.wait()


def unpack(n, blocks, arriving, received, new_keys, new_values):
    rows, lanes = new_keys.shape[1:]
    return pl.pallas_call(
        functools.partial(unpack_kernel, blocks, n),
        out_shape=[jax.ShapeDtypeStruct(x.shape, x.dtype) for x in (new_keys, new_values)],
        in_specs=[SMEM, ANY, ANY, ANY],
        out_specs=[ANY, ANY],
        input_output_aliases={2: 0, 3: 1},
        scratch_shapes=[
            pltpu.VMEM((2, n, rows, lanes), new_keys.dtype),
            pltpu.SMEM((1,), jnp.int32),
            pltpu.SemaphoreType.DMA,
            pltpu.SemaphoreType.DMA((2,)),
        ],
        name="place_moves",
    )(arriving, received, new_keys, new_values)


def attend_kernel(
    dims,
    rank_ref,
    req_ref,
    idx_ref,
    dst_ref,
    len_ref,
    dreq_ref,
    q_ref,
    k_ref,
    v_ref,
    dk_ref,
    dv_ref,
    bias_ref,
    nk_ref,
    nv_ref,
    o_ref,
    lse_ref,
    tok_ref,
    acc,
    top,
    den,
):
    blocks, width, kv, heads, hd, drafts, requests, own, aligned, steps = dims
    group = heads // kv
    qrows = heads * drafts
    i = pl.program_id(0)
    base = rank_ref[0] * blocks + i * STEP
    factor = math.log2(math.e) / math.sqrt(hd)
    nt = (((1,), (1,)), ((), ()))

    def query(r):
        q = q_ref[pl.ds(pl.multiple_of(r * drafts, drafts), drafts), :]
        return jnp.concatenate([q[:, h * hd : (h + 1) * hd] for h in range(heads)], axis=0)

    def part(s, v):
        m = jnp.max(s, axis=1, keepdims=True)
        p = jnp.exp2(s - m)
        total = jnp.sum(p, axis=1, keepdims=True)
        o = jnp.dot(p.astype(jnp.bfloat16), v, preferred_element_type=jnp.float32)
        return m, total, o

    def merge(r, m, total, o):
        old = top[r]
        new = jnp.maximum(old, m)
        a, b = jnp.exp2(old - new), jnp.exp2(m - new)
        top[r] = new
        den[r] = den[r] * a + total * b
        acc[r] = acc[r] * a + o * b

    @pl.when(i == 0)
    def _():
        row = lax.broadcasted_iota(jnp.int32, (qrows, kv * width), 0)
        col = lax.broadcasted_iota(jnp.int32, (qrows, kv * width), 1)
        tok_ref[...] = jnp.where(row // (group * drafts) == col % kv, col // kv, width)
        top[...] = jnp.full_like(top, NEG)
        den[...] = jnp.zeros_like(den)
        acc[...] = jnp.zeros_like(acc)
        for x in range(own):
            r = dreq_ref[x]
            place = x * drafts if aligned else pl.multiple_of(r * drafts, drafts)
            dk = dk_ref[pl.ds(place, drafts), :]
            dv = dv_ref[pl.ds(place, drafts), :]
            dk = jnp.concatenate([dk[:, g * hd : (g + 1) * hd] for g in range(kv)], axis=0)
            dv = jnp.concatenate([dv[:, g * hd : (g + 1) * hd] for g in range(kv)], axis=0)
            s = lax.dot_general(query(r), dk, nt, preferred_element_type=jnp.float32) * factor
            merge(r, *part(jnp.where(bias_ref[x] < 0, NEG, s), dv))

    for lo in range(0, STEP, TOGETHER):
        found = []
        for b in range(lo, lo + TOGETHER):
            r, x = req_ref[base + b], idx_ref[base + b]
            count = jnp.where(x >= 0, jnp.clip(len_ref[r] - x * width, 0, width), 0)
            s = lax.dot_general(query(r), k_ref[b], nt, preferred_element_type=jnp.float32) * factor
            s = jnp.where(tok_ref[...] < count, s, NEG)
            found.append((r,) + part(s, v_ref[b]))
        for r, m, total, o in found:
            merge(r, m, total, o)
    for b in range(STEP):
        away = dst_ref[base + b] >= 0

        @pl.when(away)
        def _():
            nk_ref[b] = jnp.zeros_like(nk_ref[b])
            nv_ref[b] = jnp.zeros_like(nv_ref[b])

        @pl.when(jnp.logical_not(away))
        def _():
            nk_ref[b] = k_ref[b]
            nv_ref[b] = v_ref[b]

    @pl.when(i == steps - 1)
    def _():
        lane = lax.broadcasted_iota(jnp.int32, (drafts, hd), 1)
        if o_ref.shape[0] > requests * drafts:
            rest = pl.ds(requests * drafts, o_ref.shape[0] - requests * drafts)
            o_ref[rest, :] = jnp.zeros_like(o_ref[rest, :])
            lse_ref[rest, :] = jnp.zeros_like(lse_ref[rest, :])

        def close(r, _):
            m, total = top[r], den[r]
            dead = total <= 0
            o = acc[r] * jnp.where(dead, 0.0, 1.0 / jnp.where(dead, 1.0, total))
            level = jnp.where(dead, NEG, m + jnp.log2(jnp.where(dead, 1.0, total)))
            rows = pl.ds(pl.multiple_of(r * drafts, drafts), drafts)
            packed = jnp.full((drafts, hd), NEG, jnp.float32)
            for h in range(heads):
                o_ref[rows, h * hd : (h + 1) * hd] = o[h * drafts : (h + 1) * drafts].astype(jnp.bfloat16)
                packed = jnp.where(lane == h, level[h * drafts : (h + 1) * drafts], packed)
            lse_ref[rows, :] = packed
            return 0

        lax.fori_loop(0, requests, close, 0)


def attend(n, rank, tables, dreq, q_all, keys, values, dk, dv, bias, kv, drafts, out_rows, aligned):
    blocks, rows, hd = keys.shape
    width = rows // kv
    block_req, block_idx, move_dst, lengths = tables
    requests = lengths.shape[0]
    heads = q_all.shape[1] // hd
    steps = blocks // STEP
    qrows = heads * drafts
    own = bias.shape[0]
    dims = (blocks, width, kv, heads, hd, drafts, requests, own, aligned, steps)
    whole = lambda x: pl.BlockSpec(x.shape, lambda i, *_: (0,) * x.ndim)
    slab = pl.BlockSpec((STEP, rows, hd), lambda i, *_: (i, 0, 0))
    grown = jax.ShapeDtypeStruct((blocks + n, rows, hd), keys.dtype)
    o = jax.ShapeDtypeStruct((out_rows, heads * hd), jnp.bfloat16)
    lse = jax.ShapeDtypeStruct((out_rows, hd), jnp.float32)
    return pl.pallas_call(
        functools.partial(attend_kernel, dims),
        out_shape=[grown, grown, o, lse],
        grid_spec=pltpu.PrefetchScalarGridSpec(
            num_scalar_prefetch=6,
            grid=(steps,),
            in_specs=[whole(q_all), slab, slab, whole(dk), whole(dv), whole(bias)],
            out_specs=[slab, slab, whole(o), whole(lse)],
            scratch_shapes=[
                pltpu.VMEM((qrows, rows), jnp.int32),
                pltpu.VMEM((requests, qrows, hd), jnp.float32),
                pltpu.VMEM((requests, qrows, hd), jnp.float32),
                pltpu.VMEM((requests, qrows, hd), jnp.float32),
            ],
        ),
        compiler_params=pltpu.CompilerParams(dimension_semantics=("arbitrary",)),
        cost_estimate=pl.CostEstimate(
            flops=4 * blocks * qrows * rows * hd, bytes_accessed=8 * blocks * rows * hd, transcendentals=0
        ),
        name="attend",
    )(rank, block_req, block_idx, move_dst, lengths, dreq, q_all, keys, values, dk, dv, bias)


def merge_parts(parts, out, level_out, heads, hd):
    levels = [level for _, level in parts]
    best = functools.reduce(jnp.maximum, levels)
    weights = [jnp.exp2(x - best) for x in levels]
    mass = functools.reduce(jnp.add, weights)
    norm = 1.0 / mass
    weights = [x * norm for x in weights]
    for h in range(heads):
        cols = slice(h * hd, (h + 1) * hd)
        total = None
        for (view, _), weight in zip(parts, weights):
            term = weight[:, h : h + 1] * view[:, cols].astype(jnp.float32)
            total = term if total is None else total + term
        out[:, cols] = total.astype(jnp.bfloat16)
    if level_out is not None:
        level_out[...] = best + jnp.log2(mass)


def combine_kernel(
    dims, o_ref, lse_ref, w_ref, out_ref, near_o, near_l, pair_o, pair_l, far_o, far_l, attn_own, attn, part, got, mix, *sems
):
    n, nh, chunk, heads, hd, rows = dims
    nos, nor, nls, nlr, fos, fo_r, fls, flr, hs, hr, ds, dr, ps, pr, local = sems
    half = n // 2
    me = lax.axis_index("ctx")
    hme = lax.axis_index("head")
    row, side = me // 2, lax.rem(me, 2)
    partner = row * 2 + 1 - side
    greet([("ctx", n), ("head", nh)])
    order = list(range(1, half)) + [0]
    sends = []

    def near(d):
        c = lax.rem(row + d, half) * 2 + 1 - side
        return (
            remote(lse_ref.at[c], near_l.at[d], nls.at[d], nlr.at[d], "ctx", partner),
            remote(o_ref.at[c], near_o.at[d], nos.at[d], nor.at[d], "ctx", partner),
        )

    def far(d):
        to = lax.rem(row + d, half) * 2 + side
        return (
            remote(pair_l.at[d], far_l.at[d], fls.at[d], flr.at[d], "ctx", to),
            remote(pair_o.at[d], far_o.at[d], fos.at[d], fo_r.at[d], "ctx", to),
        )

    for d in order:
        for c in near(d):
            c.start()
            sends.append(c)
    for d in range(1, half):
        for c in near(d):
            c.wait_recv()
        at = lax.rem(row + d, half) * 2 + side
        merge_parts(
            [(o_ref.at[at], lse_ref[at]), (near_o.at[d], near_l[d])], pair_o.at[d], pair_l.at[d], heads, hd
        )
        for c in far(d):
            c.start()
            sends.append(c)
    for c in near(0):
        c.wait_recv()
    for d in range(1, half):
        for c in far(d):
            c.wait_recv()
    merge_parts(
        [(o_ref.at[me], lse_ref[me]), (near_o.at[0], near_l[0])]
        + [(far_o.at[d], far_l[d]) for d in range(1, half)],
        attn_own,
        None,
        heads,
        hd,
    )
    mine = pltpu.make_async_copy(attn_own, attn.at[me], local)
    mine.start()

    def direct(d):
        to = lax.rem(row + d, half) * 2 + side
        return remote(attn_own, attn.at[me], ds.at[d], dr.at[d], "ctx", to)

    def landed(d, other):
        origin = lax.rem(row + half - d, half) * 2 + (1 - side if other else side)
        sem = (ps, pr) if other else (ds, dr)
        remote(attn_own, attn.at[origin], sem[0].at[d], sem[1].at[d], "ctx", partner).wait_recv()

    for d in range(1, half):
        c = direct(d)
        c.start()
        sends.append(c)
    c = remote(attn_own, attn.at[me], ps.at[0], pr.at[0], "ctx", partner)
    c.start()
    sends.append(c)

    def pass_on(d):
        landed(d, False)
        origin = lax.rem(row + half - d, half) * 2 + side
        c = remote(attn.at[origin], attn.at[origin], ps.at[d], pr.at[d], "ctx", partner)
        c.start()
        sends.append(c)

    w = w_ref[...]

    def project(j):
        e = lax.rem(j + nh - hme, nh)
        value = jnp.dot(
            attn_rows(attn, pl.multiple_of(j * rows, 16), rows, chunk), w, preferred_element_type=jnp.float32
        )

        @pl.when(e == 0)
        def _():
            mix[...] = value

        @pl.when(e != 0)
        def _():
            part[e] = value.astype(jnp.bfloat16)
            remote(part.at[e], got.at[e], hs.at[e], hr.at[e], "head", j).start()

    mine.wait()
    if rows == 2 * chunk and nh == half:
        for d in range(half):
            if d + 1 < half:
                pass_on(d + 1)
            landed(d, True)
            project(lax.rem(row + half - d, half))
    else:
        for d in range(1, half):
            pass_on(d)
        for d in range(half):
            landed(d, True)
        for d in range(nh):
            project(lax.rem(hme + 1 + d, nh))
    total = mix[...]
    for e in range(1, nh):
        c = remote(part.at[e], got.at[e], hs.at[e], hr.at[e], "head", lax.rem(hme + e, nh))
        c.wait_recv()
        sends.append(c)
        total += got[e].astype(jnp.float32)
    out_ref[...] = total.astype(jnp.bfloat16)
    for c in sends:
        c.wait_send()


def attn_rows(attn, start, rows, chunk):
    piece = math.gcd(rows, chunk)
    out = []
    for x in range(rows // piece):
        at = start + x * piece
        out.append(attn[at // chunk, pl.ds(pl.multiple_of(lax.rem(at, chunk), 16), piece), :])
    return jnp.concatenate(out, axis=0)


def combine(n, nh, o, lse, w, tokens):
    _, chunk, cols = o.shape
    hd = lse.shape[2]
    heads = cols // hd
    rows = tokens // nh
    wide = w.shape[1]
    half = n // 2
    dims = (n, nh, chunk, heads, hd, rows)
    dma = pltpu.SemaphoreType.DMA
    outs = pltpu.VMEM((half, chunk, cols), jnp.bfloat16)
    levels = pltpu.VMEM((half, chunk, hd), jnp.float32)
    return pl.pallas_call(
        functools.partial(combine_kernel, dims),
        out_shape=jax.ShapeDtypeStruct((rows, wide), jnp.bfloat16),
        in_specs=[VMEM] * 3,
        out_specs=VMEM,
        scratch_shapes=[outs, levels] * 3
        + [
            pltpu.VMEM((chunk, cols), jnp.bfloat16),
            pltpu.VMEM((n, chunk, cols), jnp.bfloat16),
            pltpu.VMEM((nh, rows, wide), jnp.bfloat16),
            pltpu.VMEM((nh, rows, wide), jnp.bfloat16),
            pltpu.VMEM((rows, wide), jnp.float32),
        ]
        + [dma((half,))] * 8
        + [dma((nh,))] * 2
        + [dma((half,))] * 4
        + [dma],
        compiler_params=pltpu.CompilerParams(collective_id=1, has_side_effects=True),
        name="combine",
    )(o, lse, w)


def shards(
    n,
    nh,
    queries,
    draft_keys,
    draft_values,
    cache_keys,
    cache_values,
    w_out,
    lengths,
    block_req,
    block_idx,
    move_dst,
    draft_offs,
):
    blocks, width, kv, hd = cache_keys.shape
    requests, drafts = draft_offs.shape
    tokens = requests * drafts
    local_tokens = queries.shape[0]
    heads = queries.shape[1] // hd
    me = lax.axis_index("ctx")
    rank = jnp.reshape(me, (1,)).astype(jnp.int32)
    keys = cache_keys.reshape(blocks, width * kv, hd)
    values = cache_values.reshape(blocks, width * kv, hd)
    sent = pack(n, rank, move_dst, keys, values)
    arriving = jnp.sum((move_dst.reshape(n, blocks) == me).astype(jnp.int32), axis=1)

    aligned = local_tokens % drafts == 0
    if aligned:
        own = local_tokens // drafts
        dreq = me * own + jnp.arange(own, dtype=jnp.int32)
        valid = jnp.full((own,), True)
        (q_all,) = gather_all(n, [queries])
        dk, dv = draft_keys, draft_values
    else:
        own = -(-requests // n)
        dreq = me + n * jnp.arange(own, dtype=jnp.int32)
        valid = dreq < requests
        dreq = jnp.where(valid, dreq, 0)
        q_all, dk, dv = gather_all(n, [queries, draft_keys, draft_values])
        dk, dv = dk.reshape(tokens, -1), dv.reshape(tokens, -1)
    sent, q_all = lax.optimization_barrier((sent, q_all))
    received = lax.all_to_all(sent, "ctx", split_axis=0, concat_axis=0, tiled=True)
    q_all = q_all.reshape(tokens, heads * hd)
    offs = jnp.take(draft_offs, dreq, axis=0)
    line = jnp.arange(drafts, dtype=jnp.int32)
    seen = (line[None, None, :] >= offs[:, :, None]) & (line[None, None, :] <= line[None, :, None])
    seen = seen & valid[:, None, None]
    same = jnp.arange(heads)[:, None] // (heads // kv) == jnp.arange(kv)[None, :]
    bias = jnp.where(
        seen[:, None, :, None, :] & same[None, :, None, :, None], 0.0, -1.0
    ).astype(jnp.float32).reshape(own, heads * drafts, kv * drafts)
    chunk = -(-requests // n) * drafts
    new_keys, new_values, o, lse = attend(
        n,
        rank,
        (block_req, block_idx, move_dst, lengths),
        dreq,
        q_all,
        keys,
        values,
        dk,
        dv,
        bias,
        kv,
        drafts,
        n * chunk,
        aligned,
    )
    mixed = combine(n, nh, o.reshape(n, chunk, -1), lse.reshape(n, chunk, -1), w_out, tokens)
    new_keys, new_values = unpack(n, blocks, arriving, received, new_keys, new_values)
    shape = (blocks + n, width, kv, hd)
    return (mixed, new_keys.reshape(shape), new_values.reshape(shape))


def solution(mesh):
    in_specs = (
        P("ctx", "head"),
        P("ctx", "head"),
        P("ctx", "head"),
        P("ctx", None, "head", None),
        P("ctx", None, "head", None),
        P("head", "ctx"),
        P(),
        P(),
        P(),
        P(),
        P(),
    )
    out_specs = (P("head", "ctx"), P("ctx", None, "head", None), P("ctx", None, "head", None))
    body = functools.partial(shards, mesh.shape["ctx"], mesh.shape["head"])
    return jax.shard_map(body, mesh=mesh, in_specs=in_specs, out_specs=out_specs, check_vma=False)
```

```python
import functools
import math

import jax
import jax.numpy as jnp
from jax import lax
from jax.experimental import pallas as pl
from jax.experimental.pallas import tpu as pltpu
from jax.sharding import PartitionSpec as P

CAP = 2
STEP = 8
TOGETHER = 4
NEG = -1e30
MESH = pl.DeviceIdType.MESH
VMEM = pl.BlockSpec(memory_space=pltpu.VMEM)
SMEM = pl.BlockSpec(memory_space=pltpu.SMEM)
ANY = pl.BlockSpec(memory_space=pl.ANY)


def greet(axes):
    barrier = pltpu.get_barrier_semaphore()
    total = 0
    for axis, size in axes:
        me = lax.axis_index(axis)
        for d in range(1, size):
            pl.semaphore_signal(
                barrier, inc=1, device_id={axis: lax.rem(me + d, size)}, device_id_type=MESH
            )
        total += size - 1
    pl.semaphore_wait(barrier, total)


def remote(src, dst, send, recv, axis, to):
    return pltpu.make_async_remote_copy(
        src_ref=src, dst_ref=dst, send_sem=send, recv_sem=recv, device_id={axis: to}, device_id_type=MESH
    )


def spread(n, parts, send_sem, recv_sem, pair_send, pair_recv):
    me = lax.axis_index("ctx")
    half = n // 2
    row, side = me // 2, lax.rem(me, 2)
    partner = row * 2 + 1 - side
    started = []
    for a, (src, dst) in enumerate(parts):
        for d in range(1, half):
            to = lax.rem(row + d, half) * 2 + side
            c = remote(src, dst(me), send_sem.at[a, d], recv_sem.at[a, d], "ctx", to)
            c.start()
            started.append(c)
        c = remote(src, dst(me), pair_send.at[a, 0], pair_recv.at[a, 0], "ctx", partner)
        c.start()
        started.append(c)
    for d in range(1, half):
        for a, (src, dst) in enumerate(parts):
            origin = lax.rem(row + half - d, half) * 2 + side
            remote(src, dst(origin), send_sem.at[a, d], recv_sem.at[a, d], "ctx", partner).wait_recv()
            c = remote(
                dst(origin), dst(origin), pair_send.at[a, d], pair_recv.at[a, d], "ctx", partner
            )
            c.start()
            started.append(c)
    for d in range(half):
        for a, (src, dst) in enumerate(parts):
            origin = lax.rem(row + half - d, half) * 2 + 1 - side
            remote(src, dst(origin), pair_send.at[a, d], pair_recv.at[a, d], "ctx", partner).wait_recv()
    for c in started:
        c.wait_send()


def spread_sems(n, count):
    half = n // 2
    return [pltpu.SemaphoreType.DMA((count, half))] * 4


def pieces(width):
    if width % 256:
        return [slice(0, width)]
    return [slice(0, width // 2), slice(width // 2, width)]


def gather_kernel(n, count, *refs):
    srcs, dsts, sems = refs[:count], refs[count : 2 * count], refs[2 * count :]
    local = sems[4]
    greet([("ctx", n)])
    me = lax.axis_index("ctx")
    own = []
    for a in range(count):
        c = pltpu.make_async_copy(srcs[a], dsts[a].at[me], local.at[a])
        c.start()
        own.append(c)
    parts = []
    for src, dst in zip(srcs, dsts):
        for cols in pieces(src.shape[1]):
            parts.append((src.at[:, cols], lambda o, dst=dst, cols=cols: dst.at[o, :, cols]))
    spread(n, parts, *sems[:4])
    for c in own:
        c.wait()


def gather_all(n, arrays):
    count = len(arrays)
    return pl.pallas_call(
        functools.partial(gather_kernel, n, count),
        out_shape=[jax.ShapeDtypeStruct((n,) + x.shape, x.dtype) for x in arrays],
        in_specs=[VMEM] * count,
        out_specs=[VMEM] * count,
        scratch_shapes=spread_sems(n, sum(len(pieces(x.shape[1])) for x in arrays))
        + [pltpu.SemaphoreType.DMA((count,))],
        compiler_params=pltpu.CompilerParams(collective_id=0, has_side_effects=True),
        name="gather_queries",
    )(*arrays)


def pack_kernel(blocks, n, rank_ref, dst_ref, k_ref, v_ref, out_ref, seen, sem):
    base = rank_ref[0] * blocks
    for d in range(n):
        seen[d] = 0

    def start(s, _):
        d = dst_ref[base + s]

        @pl.when(d >= 0)
        def _():
            row = d * CAP + seen[d]
            seen[d] = seen[d] + 1
            pltpu.make_async_copy(k_ref.at[s], out_ref.at[row, 0], sem).start()
            pltpu.make_async_copy(v_ref.at[s], out_ref.at[row, 1], sem).start()

        return 0

    lax.fori_loop(0, blocks, start, 0)

    def finish(s, _):
        @pl.when(dst_ref[base + s] >= 0)
        def _():
            pltpu.make_async_copy(k_ref.at[0], out_ref.at[0, 0], sem).wait()
            pltpu.make_async_copy(v_ref.at[0], out_ref.at[0, 1], sem).wait()

        return 0

    lax.fori_loop(0, blocks, finish, 0)


def pack(n, rank, move_dst, keys, values):
    blocks, rows, lanes = keys.shape
    return pl.pallas_call(
        functools.partial(pack_kernel, blocks, n),
        out_shape=jax.ShapeDtypeStruct((n * CAP, 2, rows, lanes), keys.dtype),
        in_specs=[SMEM, SMEM, ANY, ANY],
        out_specs=VMEM,
        scratch_shapes=[pltpu.SMEM((n,), jnp.int32), pltpu.SemaphoreType.DMA],
        name="pack_moves",
    )(rank, move_dst, keys, values)


def unpack_kernel(blocks, n, cnt_ref, recv_ref, nk_in, nv_in, nk_ref, nv_ref, blank, at, sem):
    at[0] = 0
    blank[...] = jnp.zeros_like(blank)
    for src in range(n):
        for j in range(CAP):

            @pl.when((j < cnt_ref[src]) & (at[0] < n))
            def _():
                for a, ref in enumerate((nk_ref, nv_ref)):
                    pltpu.make_async_copy(recv_ref.at[src * CAP + j, a], ref.at[blocks + at[0]], sem).start()
                at[0] = at[0] + 1

    def clear(k, _):
        for ref in (nk_ref, nv_ref):
            pltpu.make_async_copy(blank, ref.at[blocks + k], sem).start()
        return 0

    lax.fori_loop(at[0], n, clear, 0)

    def finish(k, _):
        for ref in (nk_ref, nv_ref):
            pltpu.make_async_copy(blank, ref.at[blocks + k], sem).wait()
        return 0

    lax.fori_loop(0, n, finish, 0)


def unpack(n, blocks, arriving, received, new_keys, new_values):
    rows, lanes = new_keys.shape[1:]
    return pl.pallas_call(
        functools.partial(unpack_kernel, blocks, n),
        out_shape=[jax.ShapeDtypeStruct(x.shape, x.dtype) for x in (new_keys, new_values)],
        in_specs=[SMEM, VMEM, ANY, ANY],
        out_specs=[ANY, ANY],
        input_output_aliases={2: 0, 3: 1},
        scratch_shapes=[
            pltpu.VMEM((rows, lanes), new_keys.dtype),
            pltpu.SMEM((1,), jnp.int32),
            pltpu.SemaphoreType.DMA,
        ],
        name="place_moves",
    )(arriving, received, new_keys, new_values)


def attend_kernel(
    dims,
    rank_ref,
    req_ref,
    idx_ref,
    dst_ref,
    len_ref,
    dreq_ref,
    q_ref,
    k_ref,
    v_ref,
    dk_ref,
    dv_ref,
    bias_ref,
    nk_ref,
    nv_ref,
    o_ref,
    lse_ref,
    tok_ref,
    acc,
    top,
    den,
):
    blocks, width, kv, heads, hd, drafts, requests, own, aligned, steps = dims
    group = heads // kv
    qrows = heads * drafts
    i = pl.program_id(0)
    base = rank_ref[0] * blocks + i * STEP
    factor = math.log2(math.e) / math.sqrt(hd)
    nt = (((1,), (1,)), ((), ()))

    def query(r):
        q = q_ref[pl.ds(pl.multiple_of(r * drafts, drafts), drafts), :]
        return jnp.concatenate([q[:, h * hd : (h + 1) * hd] for h in range(heads)], axis=0)

    def part(s, v):
        m = jnp.max(s, axis=1, keepdims=True)
        p = jnp.exp2(s - m)
        total = jnp.sum(p, axis=1, keepdims=True)
        o = jnp.dot(p.astype(jnp.bfloat16), v, preferred_element_type=jnp.float32)
        return m, total, o

    def merge(r, m, total, o):
        old = top[r]
        new = jnp.maximum(old, m)
        a, b = jnp.exp2(old - new), jnp.exp2(m - new)
        top[r] = new
        den[r] = den[r] * a + total * b
        acc[r] = acc[r] * a + o * b

    @pl.when(i == 0)
    def _():
        row = lax.broadcasted_iota(jnp.int32, (qrows, kv * width), 0)
        col = lax.broadcasted_iota(jnp.int32, (qrows, kv * width), 1)
        tok_ref[...] = jnp.where(row // (group * drafts) == col % kv, col // kv, width)
        top[...] = jnp.full_like(top, NEG)
        den[...] = jnp.zeros_like(den)
        acc[...] = jnp.zeros_like(acc)
        for x in range(own):
            r = dreq_ref[x]
            place = x * drafts if aligned else pl.multiple_of(r * drafts, drafts)
            dk = dk_ref[pl.ds(place, drafts), :]
            dv = dv_ref[pl.ds(place, drafts), :]
            dk = jnp.concatenate([dk[:, g * hd : (g + 1) * hd] for g in range(kv)], axis=0)
            dv = jnp.concatenate([dv[:, g * hd : (g + 1) * hd] for g in range(kv)], axis=0)
            s = lax.dot_general(query(r), dk, nt, preferred_element_type=jnp.float32) * factor
            merge(r, *part(jnp.where(bias_ref[x] < 0, NEG, s), dv))

    for lo in range(0, STEP, TOGETHER):
        found = []
        for b in range(lo, lo + TOGETHER):
            r, x = req_ref[base + b], idx_ref[base + b]
            count = jnp.where(x >= 0, jnp.clip(len_ref[r] - x * width, 0, width), 0)
            s = lax.dot_general(query(r), k_ref[b], nt, preferred_element_type=jnp.float32) * factor
            s = jnp.where(tok_ref[...] < count, s, NEG)
            found.append((r,) + part(s, v_ref[b]))
        for r, m, total, o in found:
            merge(r, m, total, o)
    for b in range(STEP):
        away = dst_ref[base + b] >= 0

        @pl.when(away)
        def _():
            nk_ref[b] = jnp.zeros_like(nk_ref[b])
            nv_ref[b] = jnp.zeros_like(nv_ref[b])

        @pl.when(jnp.logical_not(away))
        def _():
            nk_ref[b] = k_ref[b]
            nv_ref[b] = v_ref[b]

    @pl.when(i == steps - 1)
    def _():
        lane = lax.broadcasted_iota(jnp.int32, (drafts, hd), 1)
        if o_ref.shape[0] > requests * drafts:
            rest = pl.ds(requests * drafts, o_ref.shape[0] - requests * drafts)
            o_ref[rest, :] = jnp.zeros_like(o_ref[rest, :])
            lse_ref[rest, :] = jnp.zeros_like(lse_ref[rest, :])

        def close(r, _):
            m, total = top[r], den[r]
            dead = total <= 0
            o = acc[r] * jnp.where(dead, 0.0, 1.0 / jnp.where(dead, 1.0, total))
            level = jnp.where(dead, NEG, m + jnp.log2(jnp.where(dead, 1.0, total)))
            rows = pl.ds(pl.multiple_of(r * drafts, drafts), drafts)
            packed = jnp.full((drafts, hd), NEG, jnp.float32)
            for h in range(heads):
                o_ref[rows, h * hd : (h + 1) * hd] = o[h * drafts : (h + 1) * drafts].astype(jnp.bfloat16)
                packed = jnp.where(lane == h, level[h * drafts : (h + 1) * drafts], packed)
            lse_ref[rows, :] = packed
            return 0

        lax.fori_loop(0, requests, close, 0)


def attend(n, rank, tables, dreq, q_all, keys, values, dk, dv, bias, kv, drafts, out_rows, aligned):
    blocks, rows, hd = keys.shape
    width = rows // kv
    block_req, block_idx, move_dst, lengths = tables
    requests = lengths.shape[0]
    heads = q_all.shape[1] // hd
    steps = blocks // STEP
    qrows = heads * drafts
    own = bias.shape[0]
    dims = (blocks, width, kv, heads, hd, drafts, requests, own, aligned, steps)
    whole = lambda x: pl.BlockSpec(x.shape, lambda i, *_: (0,) * x.ndim)
    slab = pl.BlockSpec((STEP, rows, hd), lambda i, *_: (i, 0, 0))
    grown = jax.ShapeDtypeStruct((blocks + n, rows, hd), keys.dtype)
    o = jax.ShapeDtypeStruct((out_rows, heads * hd), jnp.bfloat16)
    lse = jax.ShapeDtypeStruct((out_rows, hd), jnp.float32)
    return pl.pallas_call(
        functools.partial(attend_kernel, dims),
        out_shape=[grown, grown, o, lse],
        grid_spec=pltpu.PrefetchScalarGridSpec(
            num_scalar_prefetch=6,
            grid=(steps,),
            in_specs=[whole(q_all), slab, slab, whole(dk), whole(dv), whole(bias)],
            out_specs=[slab, slab, whole(o), whole(lse)],
            scratch_shapes=[
                pltpu.VMEM((qrows, rows), jnp.int32),
                pltpu.VMEM((requests, qrows, hd), jnp.float32),
                pltpu.VMEM((requests, qrows, hd), jnp.float32),
                pltpu.VMEM((requests, qrows, hd), jnp.float32),
            ],
        ),
        compiler_params=pltpu.CompilerParams(dimension_semantics=("arbitrary",)),
        cost_estimate=pl.CostEstimate(
            flops=4 * blocks * qrows * rows * hd, bytes_accessed=8 * blocks * rows * hd, transcendentals=0
        ),
        name="attend",
    )(rank, block_req, block_idx, move_dst, lengths, dreq, q_all, keys, values, dk, dv, bias)


def merge_parts(parts, out, level_out, heads, hd, after={}):
    levels = [level for _, level in parts]
    best = functools.reduce(jnp.maximum, levels)
    weights = [jnp.exp2(x - best) for x in levels]
    mass = functools.reduce(jnp.add, weights)
    norm = 1.0 / mass
    weights = [x * norm for x in weights]
    for h in range(heads):
        cols = slice(h * hd, (h + 1) * hd)
        total = None
        for (view, _), weight in zip(parts, weights):
            term = weight[:, h : h + 1] * view[:, cols].astype(jnp.float32)
            total = term if total is None else total + term
        out[:, cols] = total.astype(jnp.bfloat16)
        if cols.stop in after:
            after[cols.stop]()
    if level_out is not None:
        level_out[...] = best + jnp.log2(mass)


def combine_kernel(
    dims, o_ref, lse_ref, w_ref, out_ref, near_o, near_l, pair_o, pair_l, far_o, far_l, attn_own, attn, part, got, mix, *sems
):
    n, nh, chunk, heads, hd, rows = dims
    nos, nor, nls, nlr, fos, fo_r, fls, flr, hs, hr, ds, dr, ps, pr, local = sems
    half = n // 2
    me = lax.axis_index("ctx")
    hme = lax.axis_index("head")
    row, side = me // 2, lax.rem(me, 2)
    partner = row * 2 + 1 - side
    greet([("ctx", n), ("head", nh)])
    order = list(range(1, half)) + [0]
    sends = []

    def near(d):
        c = lax.rem(row + d, half) * 2 + 1 - side
        return (
            remote(lse_ref.at[c], near_l.at[d], nls.at[d], nlr.at[d], "ctx", partner),
            remote(o_ref.at[c], near_o.at[d], nos.at[d], nor.at[d], "ctx", partner),
        )

    def far(d):
        to = lax.rem(row + d, half) * 2 + side
        return (
            remote(pair_l.at[d], far_l.at[d], fls.at[d], flr.at[d], "ctx", to),
            remote(pair_o.at[d], far_o.at[d], fos.at[d], fo_r.at[d], "ctx", to),
        )

    for d in order:
        for c in near(d):
            c.start()
            sends.append(c)
    for d in range(1, half):
        for c in near(d):
            c.wait_recv()
        at = lax.rem(row + d, half) * 2 + side
        merge_parts(
            [(o_ref.at[at], lse_ref[at]), (near_o.at[d], near_l[d])], pair_o.at[d], pair_l.at[d], heads, hd
        )
        for c in far(d):
            c.start()
            sends.append(c)
    for c in near(0):
        c.wait_recv()
    for d in range(1, half):
        for c in far(d):
            c.wait_recv()
    cuts = pieces(heads * hd)

    def direct(d, p):
        to = lax.rem(row + d, half) * 2 + side
        return remote(
            attn_own.at[:, cuts[p]], attn.at[me, :, cuts[p]], ds.at[p, d], dr.at[p, d], "ctx", to
        )

    def landed(d, other, only=None):
        origin = lax.rem(row + half - d, half) * 2 + (1 - side if other else side)
        sem = (ps, pr) if other else (ds, dr)
        for p in range(len(cuts)) if only is None else [only]:
            there = attn.at[origin, :, cuts[p]]
            remote(there, there, sem[0].at[p, d], sem[1].at[p, d], "ctx", partner).wait_recv()

    def share(p):
        cut = cuts[p]
        for d in range(1, half):
            c = direct(d, p)
            c.start()
            sends.append(c)
        c = remote(
            attn_own.at[:, cut], attn.at[me, :, cut], ps.at[p, 0], pr.at[p, 0], "ctx", partner
        )
        c.start()
        sends.append(c)

    merge_parts(
        [(o_ref.at[me], lse_ref[me]), (near_o.at[0], near_l[0])]
        + [(far_o.at[d], far_l[d]) for d in range(1, half)],
        attn_own,
        None,
        heads,
        hd,
        {cut.stop: functools.partial(share, p) for p, cut in enumerate(cuts)},
    )
    mine = pltpu.make_async_copy(attn_own, attn.at[me], local)
    mine.start()

    def pass_on(d):
        origin = lax.rem(row + half - d, half) * 2 + side
        for p in range(len(cuts)):
            landed(d, False, p)
            there = attn.at[origin, :, cuts[p]]
            c = remote(there, there, ps.at[p, d], pr.at[p, d], "ctx", partner)
            c.start()
            sends.append(c)

    w = w_ref[...]

    def project(j):
        e = lax.rem(j + nh - hme, nh)
        value = jnp.dot(
            attn_rows(attn, pl.multiple_of(j * rows, 16), rows, chunk), w, preferred_element_type=jnp.float32
        )

        @pl.when(e == 0)
        def _():
            mix[...] = value

        @pl.when(e != 0)
        def _():
            part[e] = value.astype(jnp.bfloat16)
            remote(part.at[e], got.at[e], hs.at[e], hr.at[e], "head", j).start()

    mine.wait()
    if rows == 2 * chunk and nh == half:
        for d in range(half):
            if d + 1 < half:
                pass_on(d + 1)
            landed(d, True)
            project(lax.rem(row + half - d, half))
    else:
        for d in range(1, half):
            pass_on(d)
        for d in range(half):
            landed(d, True)
        for d in range(nh):
            project(lax.rem(hme + 1 + d, nh))
    total = mix[...]
    for e in range(1, nh):
        c = remote(part.at[e], got.at[e], hs.at[e], hr.at[e], "head", lax.rem(hme + e, nh))
        c.wait_recv()
        sends.append(c)
        total += got[e].astype(jnp.float32)
    out_ref[...] = total.astype(jnp.bfloat16)
    for c in sends:
        c.wait_send()


def attn_rows(attn, start, rows, chunk):
    piece = math.gcd(rows, chunk)
    out = []
    for x in range(rows // piece):
        at = start + x * piece
        out.append(attn[at // chunk, pl.ds(pl.multiple_of(lax.rem(at, chunk), 16), piece), :])
    return jnp.concatenate(out, axis=0)


def combine(n, nh, o, lse, w, tokens):
    _, chunk, cols = o.shape
    hd = lse.shape[2]
    heads = cols // hd
    rows = tokens // nh
    wide = w.shape[1]
    half = n // 2
    dims = (n, nh, chunk, heads, hd, rows)
    dma = pltpu.SemaphoreType.DMA
    outs = pltpu.VMEM((half, chunk, cols), jnp.bfloat16)
    levels = pltpu.VMEM((half, chunk, hd), jnp.float32)
    return pl.pallas_call(
        functools.partial(combine_kernel, dims),
        out_shape=jax.ShapeDtypeStruct((rows, wide), jnp.bfloat16),
        in_specs=[VMEM] * 3,
        out_specs=VMEM,
        scratch_shapes=[outs, levels] * 3
        + [
            pltpu.VMEM((chunk, cols), jnp.bfloat16),
            pltpu.VMEM((n, chunk, cols), jnp.bfloat16),
            pltpu.VMEM((nh, rows, wide), jnp.bfloat16),
            pltpu.VMEM((nh, rows, wide), jnp.bfloat16),
            pltpu.VMEM((rows, wide), jnp.float32),
        ]
        + [dma((half,))] * 8
        + [dma((nh,))] * 2
        + [dma((len(pieces(cols)), half))] * 4
        + [dma],
        compiler_params=pltpu.CompilerParams(collective_id=1, has_side_effects=True),
        name="combine",
    )(o, lse, w)


def shards(
    n,
    nh,
    queries,
    draft_keys,
    draft_values,
    cache_keys,
    cache_values,
    w_out,
    lengths,
    block_req,
    block_idx,
    move_dst,
    draft_offs,
):
    blocks, width, kv, hd = cache_keys.shape
    requests, drafts = draft_offs.shape
    tokens = requests * drafts
    local_tokens = queries.shape[0]
    heads = queries.shape[1] // hd
    me = lax.axis_index("ctx")
    rank = jnp.reshape(me, (1,)).astype(jnp.int32)
    keys = cache_keys.reshape(blocks, width * kv, hd)
    values = cache_values.reshape(blocks, width * kv, hd)
    sent = pack(n, rank, move_dst, keys, values)
    arriving = jnp.sum((move_dst.reshape(n, blocks) == me).astype(jnp.int32), axis=1)

    aligned = local_tokens % drafts == 0
    if aligned:
        own = local_tokens // drafts
        dreq = me * own + jnp.arange(own, dtype=jnp.int32)
        valid = None
        offs = lax.dynamic_slice_in_dim(draft_offs, me * own, own)
        (q_all,) = gather_all(n, [queries])
        dk, dv = draft_keys, draft_values
    else:
        own = -(-requests // n)
        dreq = me + n * jnp.arange(own, dtype=jnp.int32)
        valid = dreq < requests
        dreq = jnp.where(valid, dreq, 0)
        offs = jnp.take(draft_offs, dreq, axis=0)
        q_all, dk, dv = gather_all(n, [queries, draft_keys, draft_values])
        dk, dv = dk.reshape(tokens, -1), dv.reshape(tokens, -1)
    sent, q_all = lax.optimization_barrier((sent, q_all))
    received = lax.all_to_all(sent, "ctx", split_axis=0, concat_axis=0, tiled=True)
    q_all = q_all.reshape(tokens, heads * hd)
    line = jnp.arange(drafts, dtype=jnp.int32)
    seen = (line[None, None, :] >= offs[:, :, None]) & (line[None, None, :] <= line[None, :, None])
    if valid is not None:
        seen = seen & valid[:, None, None]
    same = jnp.arange(heads)[:, None] // (heads // kv) == jnp.arange(kv)[None, :]
    bias = jnp.where(
        seen[:, None, :, None, :] & same[None, :, None, :, None], 0.0, -1.0
    ).astype(jnp.float32).reshape(own, heads * drafts, kv * drafts)
    chunk = -(-requests // n) * drafts
    new_keys, new_values, o, lse = attend(
        n,
        rank,
        (block_req, block_idx, move_dst, lengths),
        dreq,
        q_all,
        keys,
        values,
        dk,
        dv,
        bias,
        kv,
        drafts,
        n * chunk,
        aligned,
    )
    mixed = combine(n, nh, o.reshape(n, chunk, -1), lse.reshape(n, chunk, -1), w_out, tokens)
    new_keys, new_values = unpack(n, blocks, arriving, received, new_keys, new_values)
    shape = (blocks + n, width, kv, hd)
    return (mixed, new_keys.reshape(shape), new_values.reshape(shape))


def solution(mesh):
    in_specs = (
        P("ctx", "head"),
        P("ctx", "head"),
        P("ctx", "head"),
        P("ctx", None, "head", None),
        P("ctx", None, "head", None),
        P("head", "ctx"),
        P(),
        P(),
        P(),
        P(),
        P(),
    )
    out_specs = (P("head", "ctx"), P("ctx", None, "head", None), P("ctx", None, "head", None))
    body = functools.partial(shards, mesh.shape["ctx"], mesh.shape["head"])
    return jax.shard_map(body, mesh=mesh, in_specs=in_specs, out_specs=out_specs, check_vma=False)
```
